32 devices in a mesh: chan: 4 (over x, core), pix: 8 (over z, y).
Axes of the slice: x: 2, y: 2, z: 4, core: 2. Of those that a mesh axis runs over, the one named last changes fastest.
Arguments:
- sky_map: bfloat16 [1024, 256, 1024], P('chan', 'pix'), may hold values from -6 to 6
- owner: int32 [256], P('pix'), may hold values from -1 to 3, as said below
- stamp_block: int32 [8, 4, 8, 2], P('pix', 'chan'), may hold values from -1 to 5, as said below
- chan_start: int32 [8, 4, 8, 2], P('pix', 'chan'), may hold values from 0 to 896
- overdensity: float32 [8, 4, 8, 2], replicated, may hold values from 0.2 to 3
- delay_gain: float32 [1024], replicated, may hold values from 0.1 to 1
Outputs:
- stack: float32 [8, 128, 1024], P('pix', 'chan')
The draws below stay inside these ranges and needn't reach their ends.
Inputs may be any that keep to these rules, and one draw needn't show every extreme that they name: `owner`: within each strip column every index 0 to 3 owns between 1 and 6 blocks, some index exactly 6; -1 marks masked blocks. `stamp_block`: A listed rank is below the number of blocks that the list's index owns in the list's strip column; -1 marks an empty slot; for some shard every list fills all 2 slots.
All inputs are finite; a program needn't handle non-finite values.
Results may differ from the reference program's by a relative error of at most 0.0043.
Values may be sent and summed in bfloat16 or wider, within the bound.
A program may use at most 128 MiB of HBM per device.

```python
import math
import jax
import jax.numpy as jnp
from jax import lax

CH = 1024
PIX = 1024
SCH = 128
BLK_DEV = 32
SCAP = 2
CAP = 6
NBLK = 256
N_CHAN = 4
N_PIX = 8


def layout(key):
    base_key = jax.random.fold_in(key, 11)
    full_shard = jax.random.randint(jax.random.fold_in(base_key, 1), (), 0, N_PIX)

    def one_source(source):
        source_key = jax.random.fold_in(base_key, 100 + source)
        key_count, key_heavy, key_order, key_fill, key_chosen = jax.random.split(source_key, 5)
        counts = jax.random.randint(key_count, (N_CHAN,), 1, CAP + 1)
        heavy_owner = jax.random.randint(key_heavy, (), 0, N_CHAN)
        counts = jnp.where(jnp.arange(N_CHAN) == heavy_owner, CAP, counts).astype(jnp.int32)
        rank_ends = jnp.cumsum(counts).astype(jnp.int32)
        block_order = jax.random.permutation(key_order, BLK_DEV).astype(jnp.int32)
        ranks = jnp.arange(BLK_DEV, dtype=jnp.int32)
        holder = jnp.sum((rank_ends[None, :] <= ranks[:, None]).astype(jnp.int32), axis=1)
        holder = jnp.where(ranks < rank_ends[-1], holder, -1).astype(jnp.int32)
        owner_local = jnp.zeros((BLK_DEV,), jnp.int32).at[block_order].set(holder)
        filled = jax.random.randint(key_fill, (N_CHAN, N_PIX), 0, SCAP + 1)
        filled = jnp.where(jnp.arange(N_PIX)[None, :] == full_shard, SCAP, filled)
        chosen = jax.random.randint(key_chosen, (N_CHAN, N_PIX, SCAP), 0, 65536) % counts[:, None, None]
        chosen = chosen.at[heavy_owner, full_shard, 0].set(CAP - 1)
        live_slot = jnp.arange(SCAP)[None, None, :] < filled[:, :, None]
        return (owner_local, jnp.where(live_slot, chosen, -1).astype(jnp.int32))
    owners, block_lists = jax.vmap(one_source)(jnp.arange(N_PIX))
    return (owners.reshape(-1), block_lists)


def draw_owner(key, part):
    return layout(key)[0]


def draw_stamp_block(key, part):
    return layout(key)[1]


def draw_chan_start(key, part):
    shape = (N_PIX, N_CHAN, N_PIX, SCAP)
    starts = jax.random.randint(jax.random.fold_in(key, 23), shape, 0, CH - SCH + 1).astype(jnp.int32)
    starts = starts.at[0, 0, 0, 0].set(CH - SCH)
    return starts.at[N_PIX - 1, N_CHAN - 1, N_PIX - 1, SCAP - 1].set(0)


def shard_levels(stream_key, shape, cuts, least, high):
    def one(position, blocks):
        heights = jax.random.uniform(jax.random.fold_in(jax.random.fold_in(stream_key, 6), position), (blocks,), jnp.float32, least / len(cuts), high / len(cuts))
        return jnp.repeat(jnp.exp(heights), shape[position] // blocks).reshape((-1,) + (1,) * (len(shape) - position - 1))

    level = one(*cuts[0])
    for cut in cuts[1:]:
        level = level * one(*cut)
    return level


def centred(own_key, dims, width, most, cuts=(), kind=jnp.bfloat16):
    drawn = width * jax.random.normal(own_key, dims, jnp.float32)
    if cuts:
        drawn = drawn * shard_levels(own_key, dims, cuts, -0.22, 0.18)
    return jnp.clip(drawn, -most, most).astype(kind)


def setup_inputs(seed: int = 0) -> dict:
    key_list = jax.random.split(jax.random.key(seed), 7)
    return {
        "sky_map": centred(key_list[0], (CH, NBLK, PIX), 1.0, 6.0, ((0, 4), (1, 8))),
        "owner": draw_owner(jax.random.fold_in(key_list[6], 71), 0),
        "stamp_block": draw_stamp_block(jax.random.fold_in(key_list[6], 71), 0),
        "chan_start": draw_chan_start(jax.random.fold_in(key_list[6], 71), 0),
        "overdensity": jnp.clip(jax.random.uniform(key_list[4], (N_PIX, N_CHAN, N_PIX, SCAP), jnp.float32, 0.2, 3.0), 0.2, 3.0),
        "delay_gain": jnp.clip(jnp.exp(jax.random.uniform(key_list[5], (CH,), jnp.float32, math.log(0.1), math.log(1.0))), 0.1, 1.0),
    }


def delay_table(size):
    mode = jnp.arange(size, dtype=jnp.int32)[:, None]
    chan_index = jnp.arange(size, dtype=jnp.int32)[None, :]
    half = size // 2
    freq = jnp.where(mode <= half, mode, mode - half)
    phase = freq * chan_index % size
    angle = phase.astype(jnp.float32) * (2.0 * math.pi / size)
    edge = 1.0 / math.sqrt(size)
    inner = math.sqrt(2.0 / size)
    return jnp.where(mode == 0, edge + 0.0 * angle, jnp.where(mode == half, edge * jnp.cos(angle), jnp.where(mode < half, inner * jnp.cos(angle), inner * jnp.sin(angle))))

def reference(sky_map, owner, stamp_block, chan_start, overdensity, delay_gain):
    basis = delay_table(CH)
    filter_matrix = jnp.dot((basis * delay_gain[:, None]).T, basis, precision=lax.Precision.HIGHEST, preferred_element_type=jnp.float32).astype(jnp.bfloat16)
    source_maps = sky_map.reshape(CH, N_PIX, BLK_DEV, PIX)
    owner_cols = owner.reshape(N_PIX, BLK_DEV)
    wide_filter = filter_matrix.astype(jnp.float32)
    block_ids = jnp.arange(BLK_DEV, dtype=jnp.int32)
    chan_ids = jnp.arange(N_CHAN, dtype=jnp.int32)

    def one_source(total, source):
        column = lax.dynamic_index_in_dim(source_maps, source, 1, False)
        owner_col = lax.dynamic_index_in_dim(owner_cols, source, 0, False)
        same_owner = owner_col[:, None] == owner_col[None, :]
        earlier = block_ids[None, :] < block_ids[:, None]
        block_rank = lax.optimization_barrier(jnp.sum((same_owner & earlier).astype(jnp.int32), axis=1))
        filtered = jnp.einsum('mk,kbp->mbp', wide_filter, column.astype(jnp.float32)).astype(jnp.bfloat16)
        rank_lists = lax.dynamic_index_in_dim(stamp_block, source, 0, False)
        first_chan = lax.dynamic_index_in_dim(chan_start, source, 0, False)
        weights = lax.dynamic_index_in_dim(overdensity, source, 0, False)
        match = (owner_col[None, None, None, :] == chan_ids[:, None, None, None]) & (block_rank[None, None, None, :] == rank_lists[:, :, :, None])
        live_slot = jnp.any(match, axis=3) & (rank_lists >= 0)
        block_index = lax.optimization_barrier(jnp.sum(jnp.where(match, block_ids[None, None, None, :], 0), axis=3)).astype(jnp.int32)

        def cut_stamp(block_one, chan_one):
            start = (chan_one.astype(jnp.int32), block_one.astype(jnp.int32), jnp.int32(0))
            return lax.dynamic_slice(filtered, start, (SCH, 1, PIX))[:, 0, :]
        stamps = jax.vmap(jax.vmap(jax.vmap(cut_stamp)))(block_index, first_chan)
        weights = jnp.where(live_slot, weights, 0.0)
        return (total + jnp.einsum('cqs,cqskp->qkp', weights.astype(jnp.float32), stamps.astype(jnp.float32)), None)
    start_total = jnp.zeros((N_PIX, SCH, PIX), jnp.float32)
    stack, unused = lax.scan(one_source, start_total, jnp.arange(N_PIX, dtype=jnp.int32))
    return stack
```

```python
import functools
import math

import jax
import jax.numpy as jnp
import numpy as np
from jax import lax
from jax.experimental import pallas as pl
from jax.experimental.pallas import tpu as pltpu
from jax.sharding import PartitionSpec as P

MESH = pl.DeviceIdType.MESH
STEP = 16
LANES = 128


def trig_tables(size):
    inner = 32
    outer = size // inner
    mode = np.arange(size // 2 + 1)
    fine = 2.0 * np.pi * ((mode[None, :] * np.arange(inner)[:, None]) % size) / size
    coarse = 2.0 * np.pi * ((mode[:, None] * inner * np.arange(outer)[None, :]) % size) / size
    left = np.concatenate([np.cos(fine), -np.sin(fine)], axis=1)
    right = np.concatenate([np.cos(coarse), np.sin(coarse)], axis=0)
    return left.astype(np.float32), right.astype(np.float32)


def filter_rows(delay_gain, first, width):
    size = delay_gain.shape[0]
    half = size // 2
    zero = jnp.zeros((1,), jnp.float32)
    even = delay_gain[: half + 1]
    odd = jnp.concatenate([zero, delay_gain[half + 1 :], zero])
    inside = jnp.concatenate([zero, jnp.ones((half - 1,), jnp.float32), zero])
    gains = jnp.stack([even + odd, (even - odd) * inside]) * (1.0 / size)
    left, right = trig_tables(size)
    scaled = jnp.concatenate([gains, gains], axis=1)[:, None, :] * left[None]
    kernels = jnp.einsum(
        "hbk,ka->hab", scaled, right, precision=lax.Precision.HIGHEST, preferred_element_type=jnp.float32
    ).reshape(2, size)
    diff = jnp.roll(kernels[0], -first)
    add = jnp.roll(kernels[1], -first)
    diff_rows = jnp.stack([jnp.roll(diff, i) for i in range(8)])
    add_rows = jnp.stack([jnp.roll(add, -i) for i in range(8)])
    return diff_rows, add_rows


def compute_kernel(shards, per_shard, stamp, block_s, start_s, weight_s, diff_ref, add_ref, sky_ref, out_ref, held, filt):
    step = pl.program_id(0)
    size = diff_ref.shape[1]
    width = held.shape[1]
    here = pl.multiple_of(step * STEP, STEP)
    held[:, pl.ds(here, STEP), :] = jnp.swapaxes(sky_ref[...], 0, 1)

    @pl.when(step == pl.num_programs(0) - 1)
    def _():
        @pl.loop(0, size // 8)
        def _(t):
            diff = pltpu.roll(diff_ref[...], t * 8, 1)[:, :width]
            add = pltpu.roll(add_ref[...], size - t * 8, 1)[:, :width]
            rows = (diff + add).astype(jnp.bfloat16).astype(jnp.float32)
            for h in range(width // LANES):
                filt[h, pl.ds(pl.multiple_of(t * 8, 8), 8), :] = rows[:, h * LANES : (h + 1) * LANES]

        pixels = held.shape[2]
        tile = 256

        @pl.loop(0, shards)
        def _(q):
            for n in range(pixels // tile):
                total = jnp.zeros((stamp, tile), jnp.float32)
                for j in range(per_shard):
                    slot = q * per_shard + j
                    halves = [filt[h, pl.ds(start_s[slot], stamp), :] for h in range(width // LANES)]
                    rows = jnp.concatenate(halves, axis=1).astype(jnp.bfloat16)
                    columns = held[block_s[slot], :, n * tile : (n + 1) * tile]
                    total += weight_s[slot] * jnp.dot(rows, columns, preferred_element_type=jnp.float32)
                out_ref[q, :, n * tile : (n + 1) * tile] = total.astype(jnp.bfloat16)


def reduce_kernel(groups, shards, part_ref, out_ref, near, mid, far, send1, recv1, send2, recv2):
    k = lax.axis_index("chan")
    p = lax.axis_index("pix")
    rows = out_ref.shape[0]
    barrier = pltpu.get_barrier_semaphore()
    for e in range(1, groups):
        pl.semaphore_signal(barrier, inc=1, device_id=(lax.rem(k + e, groups), p), device_id_type=MESH)
    for d in range(1, shards):
        pl.semaphore_signal(barrier, inc=1, device_id=(k, lax.rem(p + d, shards)), device_id_type=MESH)
    pl.semaphore_wait(barrier, groups + shards - 2)

    order = list(range(1, shards)) + [0]

    def first(d, e):
        q = lax.rem(p + d, shards)
        to = lax.rem(k + e, groups)
        return pltpu.make_async_remote_copy(
            src_ref=part_ref.at[q, pl.ds(pl.multiple_of(to * rows, rows), rows)],
            dst_ref=near.at[e - 1, d],
            send_sem=send1.at[e - 1, d],
            recv_sem=recv1.at[e - 1, d],
            device_id=(to, p),
            device_id_type=MESH,
        )

    def second(d):
        return pltpu.make_async_remote_copy(
            src_ref=mid.at[d],
            dst_ref=far.at[d - 1],
            send_sem=send2.at[d],
            recv_sem=recv2.at[d],
            device_id=(k, lax.rem(p + d, shards)),
            device_id_type=MESH,
        )

    for d in order:
        for e in range(1, groups):
            first(d, e).start()
    for d in order:
        q = lax.rem(p + d, shards)
        for e in range(1, groups):
            first(d, e).wait_recv()
        total = part_ref[q, pl.ds(pl.multiple_of(k * rows, rows), rows), :].astype(jnp.float32)
        for e in range(1, groups):
            total += near[e - 1, d].astype(jnp.float32)
        if d:
            mid[d] = total.astype(jnp.bfloat16)
            second(d).start()
        else:
            out_ref[...] = total
    for d in range(1, shards):
        second(d).wait_recv()
        out_ref[...] += far[d - 1].astype(jnp.float32)
    for d in range(1, shards):
        second(d).wait_send()
    for d in order:
        for e in range(1, groups):
            first(d, e).wait_send()


def body(sky_map, owner, stamp_block, chan_start, overdensity, delay_gain, *, groups, shards):
    k = lax.axis_index("chan")
    p = lax.axis_index("pix")
    width, blocks, pixels = sky_map.shape
    stamp = 128
    rows = stamp // groups
    slots = stamp_block.shape[3]
    per_shard = groups * slots

    lists = jnp.stack([stamp_block[0, 0], chan_start[0, 0]])
    every = [lists]
    for e in range(1, groups):
        every.append(lax.ppermute(lists, "chan", [(i, (i + e) % groups) for i in range(groups)]))
    every = jnp.stack(every, axis=2)
    index = (k - jnp.arange(groups, dtype=jnp.int32)) % groups
    ranks, starts = every[0], every[1]
    block_ids = jnp.arange(blocks, dtype=jnp.int32)
    same = owner[:, None] == owner[None, :]
    earlier = block_ids[None, :] < block_ids[:, None]
    block_rank = jnp.sum((same & earlier).astype(jnp.int32), axis=1)
    match = (owner == index[:, None, None]) & (block_rank == ranks[..., None])
    match = match & (ranks >= 0)[..., None]
    block_of = jnp.sum(jnp.where(match, block_ids, 0), axis=3)
    live = jnp.any(match, axis=3)
    by_column = lax.dynamic_index_in_dim(overdensity, p, 0, False)
    weights = jnp.take(by_column, index, axis=0).transpose(1, 0, 2)
    weights = jnp.where(live, weights, 0.0)
    diff_rows, add_rows = filter_rows(delay_gain, k * width, width)

    partial = pl.pallas_call(
        functools.partial(compute_kernel, shards, per_shard, stamp),
        out_shape=jax.ShapeDtypeStruct((shards, stamp, pixels), jnp.bfloat16),
        grid_spec=pltpu.PrefetchScalarGridSpec(
            num_scalar_prefetch=3,
            grid=(width // STEP,),
            in_specs=[
                pl.BlockSpec(diff_rows.shape, lambda i, *_: (0, 0)),
                pl.BlockSpec(add_rows.shape, lambda i, *_: (0, 0)),
                pl.BlockSpec((STEP, blocks, pixels), lambda i, *_: (i, 0, 0)),
            ],
            out_specs=pl.BlockSpec((shards, stamp, pixels), lambda i, *_: (0, 0, 0)),
            scratch_shapes=[
                pltpu.VMEM((blocks, width, pixels), jnp.bfloat16),
                pltpu.VMEM((width // LANES, delay_gain.shape[0], LANES), jnp.float32),
            ],
        ),
        compiler_params=pltpu.CompilerParams(vmem_limit_bytes=48 << 20),
        name="partial_stacks",
    )(block_of.reshape(-1), starts.reshape(-1), weights.reshape(-1), diff_rows, add_rows, sky_map)

    out = pl.pallas_call(
        functools.partial(reduce_kernel, groups, shards),
        out_shape=jax.ShapeDtypeStruct((rows, pixels), jnp.float32),
        in_specs=[pl.BlockSpec(memory_space=pltpu.VMEM)],
        out_specs=pl.BlockSpec(memory_space=pltpu.VMEM),
        scratch_shapes=[
            pltpu.VMEM((groups - 1, shards, rows, pixels), jnp.bfloat16),
            pltpu.VMEM((shards, rows, pixels), jnp.bfloat16),
            pltpu.VMEM((shards - 1, rows, pixels), jnp.bfloat16),
            pltpu.SemaphoreType.DMA((groups - 1, shards)),
            pltpu.SemaphoreType.DMA((groups - 1, shards)),
            pltpu.SemaphoreType.DMA((shards,)),
            pltpu.SemaphoreType.DMA((shards,)),
        ],
        compiler_params=pltpu.CompilerParams(collective_id=0, has_side_effects=True),
        name="reduce_stacks",
    )(partial)
    return out[None]


def solution(mesh):
    in_specs = (
        P("chan", "pix", None),
        P("pix"),
        P("pix", "chan", None, None),
        P("pix", "chan", None, None),
        P(),
        P(),
    )
    run = functools.partial(body, groups=mesh.shape["chan"], shards=mesh.shape["pix"])
    return jax.shard_map(run, mesh=mesh, in_specs=in_specs, out_specs=P("pix", "chan", None), check_vma=False)
```

```python
import functools

import jax
import jax.numpy as jnp
import numpy as np
from jax import lax
from jax.experimental import pallas as pl
from jax.experimental.pallas import tpu as pltpu
from jax.sharding import PartitionSpec as P

MESH = pl.DeviceIdType.MESH
STEP = 32
LANES = 128


def filter_kernels(delay_gain):
    size = delay_gain.shape[0]
    half = size // 2
    mode = np.arange(half + 1)[:, None]
    angle = 2.0 * np.pi * ((mode * np.arange(size)[None, :]) % size) / size
    table = (np.cos(angle) / size).astype(np.float32)
    even = delay_gain[: half + 1]
    odd = jnp.pad(delay_gain[half + 1 :], (1, 1))
    mode = jnp.arange(half + 1, dtype=jnp.int32)
    inside = (mode > 0) & (mode < half)
    gains = jnp.stack([even + odd, jnp.where(inside, even - odd, 0.0)])
    return jnp.dot(gains, table, precision=lax.Precision.HIGHEST, preferred_element_type=jnp.float32)


def resolve_slots(groups, shards, slots, k, owner_s, lists_s, over_s, table, count, block_s, start_s, weight_s):
    blocks = owner_s.shape[0]
    for c in range(groups):
        count[c] = 0

    @pl.loop(0, blocks)
    def _(b):
        c = owner_s[b]

        @pl.when(c >= 0)
        def _():
            table[c * blocks + count[c]] = b
            count[c] = count[c] + 1

    for e in range(groups):
        c = lax.rem(k + groups - e, groups)

        @pl.loop(0, shards)
        def _(q):
            for s in range(slots):
                at = q * slots + s
                rank = lists_s[2 * e * shards * slots + at]
                live = (rank >= 0) & (rank < count[c])
                safe = jnp.where(live, rank, 0)
                to = (q * groups + e) * slots + s
                block_s[to] = jnp.where(live, table[c * blocks + safe], 0)
                start_s[to] = lists_s[(2 * e + 1) * shards * slots + at]
                weight_s[to] = jnp.where(live, over_s[c * shards * slots + at], 0.0)


def fill_filter(first, kernels_ref, filt):
    size = kernels_ref.shape[1]
    halves = filt.shape[0]
    row = lax.broadcasted_iota(jnp.int32, (8, size), 0)
    back = lax.rem(size - first, size)
    diff = pltpu.roll(jnp.broadcast_to(kernels_ref[0:1, :], (8, size)), back, 1)
    add = pltpu.roll(jnp.broadcast_to(kernels_ref[1:2, :], (8, size)), back, 1)
    diff_rows, add_rows = diff, add
    for i in range(1, 8):
        diff_rows = jnp.where(row == i, pltpu.roll(diff, i, 1), diff_rows)
        add_rows = jnp.where(row == i, pltpu.roll(add, size - i, 1), add_rows)
    lanes = size // LANES
    for v in range(LANES // 8):
        right = pltpu.roll(diff_rows, 8 * v, 1) if v else diff_rows
        left = pltpu.roll(add_rows, size - 8 * v, 1) if v else add_rows
        for u in range(lanes):
            for h in range(halves):
                a = (h - u) % lanes
                b = (h + u) % lanes
                rows = right[:, a * LANES : (a + 1) * LANES] + left[:, b * LANES : (b + 1) * LANES]
                rows = rows.astype(jnp.bfloat16).astype(jnp.float32)
                filt[h, u * LANES + 8 * v : u * LANES + 8 * v + 8, :] = rows


def compute_kernel(
    groups, shards, slots, stamp, owner_s, lists_s, over_s, kernels_ref, sky_ref, out_ref, held, filt, table, count,
    block_s, start_s, weight_s,
):
    step = pl.program_id(0)
    width = held.shape[1]
    per_shard = groups * slots
    k = lax.axis_index("chan")

    @pl.when(step == 0)
    def _():
        resolve_slots(groups, shards, slots, k, owner_s, lists_s, over_s, table, count, block_s, start_s, weight_s)
        fill_filter(k * width, kernels_ref, filt)

    for i in range(sky_ref.shape[0] // 16):
        here = pl.multiple_of(step * sky_ref.shape[0] + 16 * i, 16)
        held[:, pl.ds(here, 16), :] = jnp.swapaxes(sky_ref[16 * i : 16 * i + 16], 0, 1)

    @pl.when(step == pl.num_programs(0) - 1)
    def _():
        pixels = held.shape[2]
        tile = 256

        @pl.loop(0, shards)
        def _(q):
            for n in range(pixels // tile):
                total = jnp.zeros((stamp, tile), jnp.float32)
                for j in range(per_shard):
                    slot = q * per_shard + j
                    parts = [filt[h, pl.ds(start_s[slot], stamp), :] for h in range(width // LANES)]
                    rows = jnp.concatenate(parts, axis=1).astype(jnp.bfloat16)
                    columns = held[block_s[slot], :, n * tile : (n + 1) * tile]
                    total += weight_s[slot] * jnp.dot(rows, columns, preferred_element_type=jnp.float32)
                out_ref[q, :, n * tile : (n + 1) * tile] = total.astype(jnp.bfloat16)


def reduce_kernel(
    chips, shards, part_ref, out_ref, pair, mid1, near, keep, mid2, far, send0, recv0, send1, recv1, send2, recv2
):
    k = lax.axis_index("chan")
    p = lax.axis_index("pix")
    x = k // 2
    core = lax.rem(k, 2)
    other = 1 - core
    barrier = pltpu.get_barrier_semaphore()
    pl.semaphore_signal(barrier, inc=1, device_id=(x * 2 + other, p), device_id_type=MESH)
    for j in range(1, chips):
        pl.semaphore_signal(barrier, inc=1, device_id=(lax.rem(x + j, chips) * 2 + core, p), device_id_type=MESH)
    for d in range(1, shards):
        pl.semaphore_signal(barrier, inc=1, device_id=(k, lax.rem(p + d, shards)), device_id_type=MESH)
    pl.semaphore_wait(barrier, chips + shards - 1)

    def to_core(d):
        return pltpu.make_async_remote_copy(
            src_ref=part_ref.at[lax.rem(p + d, shards), :, other],
            dst_ref=pair.at[d],
            send_sem=send0.at[d],
            recv_sem=recv0.at[d],
            device_id=(x * 2 + other, p),
            device_id_type=MESH,
        )

    def to_chip(d, j):
        return pltpu.make_async_remote_copy(
            src_ref=mid1.at[d, j - 1],
            dst_ref=near.at[d, j - 1],
            send_sem=send1.at[d, j - 1],
            recv_sem=recv1.at[d, j - 1],
            device_id=(lax.rem(x + j, chips) * 2 + core, p),
            device_id_type=MESH,
        )

    def to_shard(d):
        return pltpu.make_async_remote_copy(
            src_ref=mid2.at[d],
            dst_ref=far.at[d - 1],
            send_sem=send2.at[d],
            recv_sem=recv2.at[d],
            device_id=(k, lax.rem(p + d, shards)),
            device_id_type=MESH,
        )

    def pair_sum(d, j):
        to = lax.rem(x + j, chips)
        mine = part_ref[lax.rem(p + d, shards), to, core].astype(jnp.float32)
        return mine + pair[d, to].astype(jnp.float32)

    def chip_stage(d):
        to_core(d).wait_recv()
        for j in range(1, chips):
            mid1[d, j - 1] = pair_sum(d, j).astype(jnp.bfloat16)
            to_chip(d, j).start()
        keep[d] = pair_sum(d, 0)

    def shard_stage(d):
        total = keep[d]
        for j in range(1, chips):
            to_chip(d, j).wait_recv()
            total += near[d, j - 1].astype(jnp.float32)
        if d:
            mid2[d] = total.astype(jnp.bfloat16)
            to_shard(d).start()
        else:
            out_ref[...] = total

    order = list(range(1, shards)) + [0]
    for d in order:
        to_core(d).start()
    lag = 2
    for i in range(shards + lag):
        if i < shards:
            chip_stage(order[i])
        if i >= lag:
            shard_stage(order[i - lag])
    for d in range(1, shards):
        to_shard(d).wait_recv()
        out_ref[...] += far[d - 1].astype(jnp.float32)
    for d in range(shards):
        to_core(d).wait_send()
        for j in range(1, chips):
            to_chip(d, j).wait_send()
        if d:
            to_shard(d).wait_send()


def body(sky_map, owner, stamp_block, chan_start, overdensity, delay_gain, *, groups, shards):
    p = lax.axis_index("pix")
    width, blocks, pixels = sky_map.shape
    stamp = 128
    chips = groups // 2
    rows = stamp // groups
    slots = stamp_block.shape[3]
    per_column = groups * shards * slots

    lists = jnp.concatenate([stamp_block.reshape(-1), chan_start.reshape(-1)])
    every = [lists]
    for e in range(1, groups):
        every.append(lax.ppermute(lists, "chan", [(i, (i + e) % groups) for i in range(groups)]))
    every = jnp.concatenate(every)
    by_column = lax.dynamic_index_in_dim(overdensity, p, 0, False).reshape(-1)
    kernels = filter_kernels(delay_gain)
    step = min(STEP, width)

    partial = pl.pallas_call(
        functools.partial(compute_kernel, groups, shards, slots, stamp),
        out_shape=jax.ShapeDtypeStruct((shards, stamp, pixels), jnp.bfloat16),
        grid_spec=pltpu.PrefetchScalarGridSpec(
            num_scalar_prefetch=3,
            grid=(width // step,),
            in_specs=[
                pl.BlockSpec(kernels.shape, lambda i, *_: (0, 0)),
                pl.BlockSpec((step, blocks, pixels), lambda i, *_: (i, 0, 0)),
            ],
            out_specs=pl.BlockSpec((shards, stamp, pixels), lambda i, *_: (0, 0, 0)),
            scratch_shapes=[
                pltpu.VMEM((blocks, width, pixels), jnp.bfloat16),
                pltpu.VMEM((width // LANES, delay_gain.shape[0], LANES), jnp.float32),
                pltpu.SMEM((groups * blocks,), jnp.int32),
                pltpu.SMEM((groups,), jnp.int32),
                pltpu.SMEM((per_column,), jnp.int32),
                pltpu.SMEM((per_column,), jnp.int32),
                pltpu.SMEM((per_column,), jnp.float32),
            ],
        ),
        compiler_params=pltpu.CompilerParams(vmem_limit_bytes=48 << 20),
        name="partial_stacks",
    )(owner, every, by_column, kernels, sky_map)

    dma = pltpu.SemaphoreType.DMA
    out = pl.pallas_call(
        functools.partial(reduce_kernel, chips, shards),
        out_shape=jax.ShapeDtypeStruct((rows, pixels), jnp.float32),
        in_specs=[pl.BlockSpec(memory_space=pltpu.VMEM)],
        out_specs=pl.BlockSpec(memory_space=pltpu.VMEM),
        scratch_shapes=[
            pltpu.VMEM((shards, chips, rows, pixels), jnp.bfloat16),
            pltpu.VMEM((shards, chips - 1, rows, pixels), jnp.bfloat16),
            pltpu.VMEM((shards, chips - 1, rows, pixels), jnp.bfloat16),
            pltpu.VMEM((shards, rows, pixels), jnp.float32),
            pltpu.VMEM((shards, rows, pixels), jnp.bfloat16),
            pltpu.VMEM((shards - 1, rows, pixels), jnp.bfloat16),
            dma((shards,)),
            dma((shards,)),
            dma((shards, chips - 1)),
            dma((shards, chips - 1)),
            dma((shards,)),
            dma((shards,)),
        ],
        compiler_params=pltpu.CompilerParams(collective_id=0, has_side_effects=True),
        name="reduce_stacks",
    )(partial.reshape(shards, chips, 2, rows, pixels))
    return out[None]


def solution(mesh):
    in_specs = (
        P("chan", "pix", None),
        P("pix"),
        P("pix", "chan", None, None),
        P("pix", "chan", None, None),
        P(),
        P(),
    )
    run = functools.partial(body, groups=mesh.shape["chan"], shards=mesh.shape["pix"])
    return jax.shard_map(run, mesh=mesh, in_specs=in_specs, out_specs=P("pix", "chan", None), check_vma=False)
```

```python
import functools

import jax
import jax.numpy as jnp
import numpy as np
from jax import lax
from jax.experimental import pallas as pl
from jax.experimental.pallas import tpu as pltpu
from jax.sharding import PartitionSpec as P

MESH = pl.DeviceIdType.MESH
STEP = 32
LANES = 128
LAG1 = 2
LAG2 = 4


def filter_kernels(delay_gain):
    size = delay_gain.shape[0]
    half = size // 2
    mode = np.arange(half + 1)[:, None]
    angle = 2.0 * np.pi * ((mode * np.arange(size)[None, :]) % size) / size
    table = (np.cos(angle) / size).astype(np.float32)
    even = delay_gain[: half + 1]
    odd = jnp.pad(delay_gain[half + 1 :], (1, 1))
    mode = jnp.arange(half + 1, dtype=jnp.int32)
    inside = (mode > 0) & (mode < half)
    gains = jnp.stack([even + odd, jnp.where(inside, even - odd, 0.0)])
    return jnp.dot(gains, table, precision=lax.Precision.HIGHEST, preferred_element_type=jnp.float32)


def resolve_kernel(owner_s, ranks_s, starts_s, out_s, table):
    c = lax.axis_index("chan")
    shards, slots = ranks_s.shape

    def fill(b, count):
        table[count] = b
        return count + (owner_s[b] == c).astype(jnp.int32)

    count = lax.fori_loop(0, owner_s.shape[0], fill, jnp.int32(0))
    for q in range(shards):
        for s in range(slots):
            rank = ranks_s[q, s]
            live = (rank >= 0) & (rank < count)
            out_s[q * slots + s] = jnp.where(live, table[jnp.where(live, rank, 0)], -1)
            out_s[(shards + q) * slots + s] = starts_s[q, s]


def fill_filter(first, kernels_ref, filt):
    size = kernels_ref.shape[1]
    halves = filt.shape[0]
    row = lax.broadcasted_iota(jnp.int32, (8, size), 0)
    back = lax.rem(size - first, size)
    diff = pltpu.roll(jnp.broadcast_to(kernels_ref[0:1, :], (8, size)), back, 1)
    add = pltpu.roll(jnp.broadcast_to(kernels_ref[1:2, :], (8, size)), back, 1)
    diff_rows, add_rows = diff, add
    for i in range(1, 8):
        diff_rows = jnp.where(row == i, pltpu.roll(diff, i, 1), diff_rows)
        add_rows = jnp.where(row == i, pltpu.roll(add, size - i, 1), add_rows)
    lanes = size // LANES
    for v in range(LANES // 8):
        right = pltpu.roll(diff_rows, 8 * v, 1) if v else diff_rows
        left = pltpu.roll(add_rows, size - 8 * v, 1) if v else add_rows
        for u in range(lanes):
            for h in range(halves):
                a = (h - u) % lanes
                b = (h + u) % lanes
                rows = right[:, a * LANES : (a + 1) * LANES] + left[:, b * LANES : (b + 1) * LANES]
                rows = rows.astype(jnp.bfloat16).astype(jnp.float32)
                filt[h, u * LANES + 8 * v : u * LANES + 8 * v + 8, :] = rows


def stack_kernel(
    groups, shards, slots, stamp, lists_s, over_s, kernels_ref, sky_a, sky_b, out_ref,
    held, filt, part, pair, mid1, near, keep, mid2, far, send0, recv0, send1, recv1, send2, recv2,
):
    step = pl.program_id(0)
    width, pixels = held.shape[1:]
    chips = groups // 2
    rows = stamp // groups
    column = shards * slots
    k = lax.axis_index("chan")
    p = lax.axis_index("pix")
    x = k // 2
    core = lax.rem(k, 2)
    other = 1 - core

    @pl.when(step == 0)
    def _():
        barrier = pltpu.get_barrier_semaphore()
        pl.semaphore_signal(barrier, inc=1, device_id=(x * 2 + other, p), device_id_type=MESH)
        for j in range(1, chips):
            pl.semaphore_signal(barrier, inc=1, device_id=(lax.rem(x + j, chips) * 2 + core, p), device_id_type=MESH)
        for d in range(1, shards):
            pl.semaphore_signal(barrier, inc=1, device_id=(k, lax.rem(p + d, shards)), device_id_type=MESH)
        fill_filter(k * width, kernels_ref, filt)
        pl.semaphore_wait(barrier, chips + shards - 1)

    half = sky_a.shape[1]
    for i in range(sky_a.shape[0] // 16):
        here = pl.multiple_of(step * sky_a.shape[0] + 16 * i, 16)
        held[:half, pl.ds(here, 16), :] = jnp.swapaxes(sky_a[16 * i : 16 * i + 16], 0, 1)
        held[half:, pl.ds(here, 16), :] = jnp.swapaxes(sky_b[16 * i : 16 * i + 16], 0, 1)

    def to_core(i):
        return pltpu.make_async_remote_copy(
            src_ref=part.at[i, :, other],
            dst_ref=pair.at[i],
            send_sem=send0.at[i],
            recv_sem=recv0.at[i],
            device_id=(x * 2 + other, p),
            device_id_type=MESH,
        )

    def to_chip(i, j):
        return pltpu.make_async_remote_copy(
            src_ref=mid1.at[i, j - 1],
            dst_ref=near.at[i, j - 1],
            send_sem=send1.at[i, j - 1],
            recv_sem=recv1.at[i, j - 1],
            device_id=(lax.rem(x + j, chips) * 2 + core, p),
            device_id_type=MESH,
        )

    def to_shard(i):
        return pltpu.make_async_remote_copy(
            src_ref=mid2.at[i],
            dst_ref=far.at[i],
            send_sem=send2.at[i],
            recv_sem=recv2.at[i],
            device_id=(k, lax.rem(p + 1 + i, shards)),
            device_id_type=MESH,
        )

    def compute(i):
        q = lax.rem(p + 1 + i, shards)
        tile = 256
        for n in range(pixels // tile):
            total = jnp.zeros((stamp, tile), jnp.float32)
            for e in range(groups):
                c = lax.rem(k + groups - e, groups)
                for s in range(slots):
                    at = q * slots + s
                    block = lists_s[2 * e * column + at]
                    first = lists_s[(2 * e + 1) * column + at]
                    weight = jnp.where(block >= 0, over_s[c * column + at], 0.0)
                    parts = [filt[h, pl.ds(first, stamp), :] for h in range(width // LANES)]
                    cut = jnp.concatenate(parts, axis=1).astype(jnp.bfloat16)
                    columns = held[jnp.maximum(block, 0), :, n * tile : (n + 1) * tile]
                    total += weight * jnp.dot(cut, columns, preferred_element_type=jnp.float32)
            total = total.astype(jnp.bfloat16).reshape(chips, 2, rows, tile)
            part[i, :, :, :, n * tile : (n + 1) * tile] = total

    def pair_sum(i, j):
        to = lax.rem(x + j, chips)
        return part[i, to, core].astype(jnp.float32) + pair[i, to].astype(jnp.float32)

    def chip_stage(i):
        to_core(i).wait_recv()
        for j in range(1, chips):
            mid1[i, j - 1] = pair_sum(i, j).astype(jnp.bfloat16)
            to_chip(i, j).start()
        keep[i] = pair_sum(i, 0)

    def shard_sum(i):
        total = keep[i]
        for j in range(1, chips):
            to_chip(i, j).wait_recv()
            total += near[i, j - 1].astype(jnp.float32)
        return total

    @pl.when(step == pl.num_programs(0) - 1)
    def _():
        @pl.loop(0, shards + LAG2 - 1)
        def _(i):
            @pl.when(i < shards)
            def _():
                compute(i)
                to_core(i).start()

            @pl.when((i >= LAG1) & (i < shards + LAG1))
            def _():
                chip_stage(i - LAG1)

            @pl.when(i >= LAG2)
            def _():
                mid2[i - LAG2] = shard_sum(i - LAG2).astype(jnp.bfloat16)
                to_shard(i - LAG2).start()

        out_ref[...] = shard_sum(shards - 1)
        for i in range(shards - 1):
            to_shard(i).wait_recv()
            out_ref[...] += far[i].astype(jnp.float32)
        for i in range(shards):
            to_core(i).wait_send()
            for j in range(1, chips):
                to_chip(i, j).wait_send()
            if i < shards - 1:
                to_shard(i).wait_send()


def body(sky_map, owner, stamp_block, chan_start, overdensity, delay_gain, *, groups, shards):
    p = lax.axis_index("pix")
    width, blocks, pixels = sky_map.shape
    stamp = 128
    chips = groups // 2
    rows = stamp // groups
    slots = stamp_block.shape[3]

    smem = pl.BlockSpec(memory_space=pltpu.SMEM)
    lists = pl.pallas_call(
        resolve_kernel,
        out_shape=jax.ShapeDtypeStruct((2 * shards * slots,), jnp.int32),
        in_specs=[smem] * 3,
        out_specs=smem,
        scratch_shapes=[pltpu.SMEM((blocks + 1,), jnp.int32)],
        name="resolve_slots",
    )(owner, stamp_block[0, 0], chan_start[0, 0])
    every = [lists]
    for e in range(1, groups):
        every.append(lax.ppermute(lists, "chan", [(i, (i + e) % groups) for i in range(groups)]))
    every = jnp.concatenate(every)
    by_column = lax.dynamic_index_in_dim(overdensity, p, 0, False).reshape(-1)
    kernels = filter_kernels(delay_gain)
    step = min(STEP, width)

    dma = pltpu.SemaphoreType.DMA
    sky = (step, blocks // 2, pixels)
    out = pl.pallas_call(
        functools.partial(stack_kernel, groups, shards, slots, stamp),
        out_shape=jax.ShapeDtypeStruct((rows, pixels), jnp.float32),
        grid_spec=pltpu.PrefetchScalarGridSpec(
            num_scalar_prefetch=2,
            grid=(width // step,),
            in_specs=[
                pl.BlockSpec(kernels.shape, lambda i, *_: (0, 0)),
                pl.BlockSpec(sky, lambda i, *_: (i, 0, 0)),
                pl.BlockSpec(sky, lambda i, *_: (i, 1, 0)),
            ],
            out_specs=pl.BlockSpec((rows, pixels), lambda i, *_: (0, 0)),
            scratch_shapes=[
                pltpu.VMEM((blocks, width, pixels), jnp.bfloat16),
                pltpu.VMEM((width // LANES, delay_gain.shape[0], LANES), jnp.float32),
                pltpu.VMEM((shards, chips, 2, rows, pixels), jnp.bfloat16),
                pltpu.VMEM((shards, chips, rows, pixels), jnp.bfloat16),
                pltpu.VMEM((shards, chips - 1, rows, pixels), jnp.bfloat16),
                pltpu.VMEM((shards, chips - 1, rows, pixels), jnp.bfloat16),
                pltpu.VMEM((shards, rows, pixels), jnp.float32),
                pltpu.VMEM((shards - 1, rows, pixels), jnp.bfloat16),
                pltpu.VMEM((shards - 1, rows, pixels), jnp.bfloat16),
                dma((shards,)),
                dma((shards,)),
                dma((shards, chips - 1)),
                dma((shards, chips - 1)),
                dma((shards - 1,)),
                dma((shards - 1,)),
            ],
        ),
        compiler_params=pltpu.CompilerParams(
            collective_id=0, has_side_effects=True, vmem_limit_bytes=48 << 20
        ),
        name="stack_stamps",
    )(every, by_column, kernels, sky_map, sky_map)
    return out[None]


def solution(mesh):
    in_specs = (
        P("chan", "pix", None),
        P("pix"),
        P("pix", "chan", None, None),
        P("pix", "chan", None, None),
        P(),
        P(),
    )
    run = functools.partial(body, groups=mesh.shape["chan"], shards=mesh.shape["pix"])
    return jax.shard_map(run, mesh=mesh, in_specs=in_specs, out_specs=P("pix", "chan", None), check_vma=False)
```

```python
import functools

import jax
import jax.numpy as jnp
import numpy as np
from jax import lax
from jax.experimental import pallas as pl
from jax.experimental.pallas import tpu as pltpu
from jax.sharding import PartitionSpec as P

MESH = pl.DeviceIdType.MESH
STEP = 32
LANES = 128
LAG1 = 2
LAG2 = 4


def cosine_table(size):
    mode = np.arange(size // 2)[:, None]
    angle = 2.0 * np.pi * ((mode * np.arange(size)[None, :]) % size) / size
    return (np.cos(angle) / size).astype(np.float32)


def filter_piece(gain_ref, table_ref, first):
    size = gain_ref.shape[1]
    half = size // 2
    piece = table_ref.shape[1]
    gain = jnp.broadcast_to(gain_ref[...], (8, size))
    even = gain[:, :half]
    odd = gain[:, half:]
    mode = lax.broadcasted_iota(jnp.int32, (8, half), 1)
    row = lax.broadcasted_iota(jnp.int32, (8, half), 0)
    odd = jnp.where(mode == 0, 0.0, odd)
    minus = jnp.where(mode == 0, 0.0, even - odd)
    gains = jnp.where(row == 0, even + odd, minus)
    out = jnp.dot(gains, table_ref[...], precision=lax.Precision.HIGHEST, preferred_element_type=jnp.float32)
    at = lax.broadcasted_iota(jnp.int32, (8, piece), 1) + first
    sign = jnp.where(lax.rem(at, 2) == 0, 1.0 / size, -1.0 / size)
    top = lax.broadcasted_iota(jnp.int32, (8, piece), 0) == 0
    return out + jnp.where(top, gain[:, half : half + 1] * sign, 0.0)


def resolve_kernel(owner_s, ranks_s, starts_s, out_s, table):
    c = lax.axis_index("chan")
    shards, slots = ranks_s.shape

    def fill(b, count):
        table[count] = b
        return count + (owner_s[b] == c).astype(jnp.int32)

    count = lax.fori_loop(0, owner_s.shape[0], fill, jnp.int32(0))
    for q in range(shards):
        for s in range(slots):
            rank = ranks_s[q, s]
            live = (rank >= 0) & (rank < count)
            out_s[q * slots + s] = jnp.where(live, table[jnp.where(live, rank, 0)], -1)
            out_s[(shards + q) * slots + s] = starts_s[q, s]


def fill_filter(first, kernels_ref, filt):
    size = kernels_ref.shape[1]
    halves = filt.shape[0]
    row = lax.broadcasted_iota(jnp.int32, (8, size), 0)
    back = lax.rem(size - first, size)
    diff = pltpu.roll(jnp.broadcast_to(kernels_ref[0:1, :], (8, size)), back, 1)
    add = pltpu.roll(jnp.broadcast_to(kernels_ref[1:2, :], (8, size)), back, 1)
    diff_rows, add_rows = diff, add
    for i in range(1, 8):
        diff_rows = jnp.where(row == i, pltpu.roll(diff, i, 1), diff_rows)
        add_rows = jnp.where(row == i, pltpu.roll(add, size - i, 1), add_rows)
    lanes = size // LANES
    for v in range(LANES // 8):
        right = pltpu.roll(diff_rows, 8 * v, 1) if v else diff_rows
        left = pltpu.roll(add_rows, size - 8 * v, 1) if v else add_rows
        for u in range(lanes):
            for h in range(halves):
                a = (h - u) % lanes
                b = (h + u) % lanes
                rows = right[:, a * LANES : (a + 1) * LANES] + left[:, b * LANES : (b + 1) * LANES]
                rows = rows.astype(jnp.bfloat16).astype(jnp.float32)
                filt[h, u * LANES + 8 * v : u * LANES + 8 * v + 8, :] = rows


def stack_kernel(
    groups, shards, slots, stamp, over_s, lists_ref, gain_ref, table_ref, sky_a, sky_b, out_ref,
    own_s, peers_s, peers, local, send_l, recv_l, kernels_ref, held, filt, part, pair, mid1, near, keep, mid2, far, send0, recv0, send1, recv1, send2, recv2,
):
    step = pl.program_id(0)
    width, pixels = held.shape[1:]
    chips = groups // 2
    rows = stamp // groups
    column = shards * slots
    k = lax.axis_index("chan")
    p = lax.axis_index("pix")
    x = k // 2
    core = lax.rem(k, 2)
    other = 1 - core

    def to_peer(e):
        return pltpu.make_async_remote_copy(
            src_ref=lists_ref,
            dst_ref=peers.at[pl.ds(e - 1, 1)],
            send_sem=send_l.at[e - 1],
            recv_sem=recv_l.at[e - 1],
            device_id=(lax.rem(k + e, groups), p),
            device_id_type=MESH,
        )

    own_lists = pltpu.make_async_copy(lists_ref, own_s, local.at[0])
    peer_lists = pltpu.make_async_copy(peers, peers_s, local.at[1])

    @pl.when(step == 0)
    def _():
        barrier = pltpu.get_barrier_semaphore()
        for e in range(1, groups):
            pl.semaphore_signal(barrier, inc=1, device_id=(lax.rem(k + e, groups), p), device_id_type=MESH)
        for d in range(1, shards):
            pl.semaphore_signal(barrier, inc=1, device_id=(k, lax.rem(p + d, shards)), device_id_type=MESH)

    @pl.when(step == 2)
    def _():
        pl.semaphore_wait(pltpu.get_barrier_semaphore(), groups + shards - 2)
        own_lists.start()
        for e in range(1, groups):
            to_peer(e).start()

    piece = table_ref.shape[1]
    lane = pl.multiple_of(step * piece, piece)
    kernels_ref[:, pl.ds(lane, piece)] = filter_piece(gain_ref, table_ref, lane)

    half = sky_a.shape[1]
    for i in range(sky_a.shape[0] // 16):
        here = pl.multiple_of(step * sky_a.shape[0] + 16 * i, 16)
        held[:half, pl.ds(here, 16), :] = jnp.swapaxes(sky_a[16 * i : 16 * i + 16], 0, 1)
        held[half:, pl.ds(here, 16), :] = jnp.swapaxes(sky_b[16 * i : 16 * i + 16], 0, 1)

    def to_core(i):
        return pltpu.make_async_remote_copy(
            src_ref=part.at[i, :, other],
            dst_ref=pair.at[i],
            send_sem=send0.at[i],
            recv_sem=recv0.at[i],
            device_id=(x * 2 + other, p),
            device_id_type=MESH,
        )

    def to_chip(i, j):
        return pltpu.make_async_remote_copy(
            src_ref=mid1.at[i, j - 1],
            dst_ref=near.at[i, j - 1],
            send_sem=send1.at[i, j - 1],
            recv_sem=recv1.at[i, j - 1],
            device_id=(lax.rem(x + j, chips) * 2 + core, p),
            device_id_type=MESH,
        )

    def to_shard(i):
        return pltpu.make_async_remote_copy(
            src_ref=mid2.at[i],
            dst_ref=far.at[i],
            send_sem=send2.at[i],
            recv_sem=recv2.at[i],
            device_id=(k, lax.rem(p + 1 + i, shards)),
            device_id_type=MESH,
        )

    def compute(i):
        q = lax.rem(p + 1 + i, shards)
        tile = 256
        for n in range(pixels // tile):
            total = jnp.zeros((stamp, tile), jnp.float32)
            for e in range(groups):
                c = lax.rem(k + groups - e, groups)
                for s in range(slots):
                    at = q * slots + s
                    block = peers_s[e - 1, at] if e else own_s[0, at]
                    first = peers_s[e - 1, column + at] if e else own_s[0, column + at]
                    weight = jnp.where(block >= 0, over_s[c * column + at], 0.0)
                    parts = [filt[h, pl.ds(first, stamp), :] for h in range(width // LANES)]
                    cut = jnp.concatenate(parts, axis=1).astype(jnp.bfloat16)
                    columns = held[jnp.maximum(block, 0), :, n * tile : (n + 1) * tile]
                    total += weight * jnp.dot(cut, columns, preferred_element_type=jnp.float32)
            total = total.astype(jnp.bfloat16).reshape(chips, 2, rows, tile)
            part[i, :, :, :, n * tile : (n + 1) * tile] = total

    def pair_sum(i, j):
        to = lax.rem(x + j, chips)
        return part[i, to, core].astype(jnp.float32) + pair[i, to].astype(jnp.float32)

    def chip_stage(i):
        to_core(i).wait_recv()
        for j in range(1, chips):
            mid1[i, j - 1] = pair_sum(i, j).astype(jnp.bfloat16)
            to_chip(i, j).start()
        keep[i] = pair_sum(i, 0)

    def shard_sum(i):
        total = keep[i]
        for j in range(1, chips):
            to_chip(i, j).wait_recv()
            total += near[i, j - 1].astype(jnp.float32)
        return total

    @pl.when(step == pl.num_programs(0) - 1)
    def _():
        for e in range(1, groups):
            to_peer(e).wait_recv()
        peer_lists.start()
        fill_filter(k * width, kernels_ref, filt)
        own_lists.wait()
        peer_lists.wait()

        @pl.loop(0, shards + LAG2 - 1)
        def _(i):
            @pl.when(i < shards)
            def _():
                compute(i)
                to_core(i).start()

            @pl.when((i >= LAG1) & (i < shards + LAG1))
            def _():
                chip_stage(i - LAG1)

            @pl.when(i >= LAG2)
            def _():
                mid2[i - LAG2] = shard_sum(i - LAG2).astype(jnp.bfloat16)
                to_shard(i - LAG2).start()

        out_ref[...] = shard_sum(shards - 1)
        for i in range(shards - 1):
            to_shard(i).wait_recv()
            out_ref[...] += far[i].astype(jnp.float32)
        for e in range(1, groups):
            to_peer(e).wait_send()
        for i in range(shards):
            to_core(i).wait_send()
            for j in range(1, chips):
                to_chip(i, j).wait_send()
            if i < shards - 1:
                to_shard(i).wait_send()


def body(sky_map, owner, stamp_block, chan_start, overdensity, delay_gain, *, groups, shards):
    p = lax.axis_index("pix")
    width, blocks, pixels = sky_map.shape
    stamp = 128
    chips = groups // 2
    rows = stamp // groups
    slots = stamp_block.shape[3]

    smem = pl.BlockSpec(memory_space=pltpu.SMEM)
    lists = pl.pallas_call(
        resolve_kernel,
        out_shape=jax.ShapeDtypeStruct((LANES,), jnp.int32),
        in_specs=[smem] * 3,
        out_specs=smem,
        scratch_shapes=[pltpu.SMEM((blocks + 1,), jnp.int32)],
        name="resolve_slots",
    )(owner, stamp_block[0, 0], chan_start[0, 0])
    by_column = lax.dynamic_index_in_dim(overdensity, p, 0, False).reshape(-1)
    step = min(STEP, width)
    steps = width // step
    size = delay_gain.shape[0]
    piece = size // steps

    dma = pltpu.SemaphoreType.DMA
    sky = (step, blocks // 2, pixels)
    out = pl.pallas_call(
        functools.partial(stack_kernel, groups, shards, slots, stamp),
        out_shape=jax.ShapeDtypeStruct((rows, pixels), jnp.float32),
        grid_spec=pltpu.PrefetchScalarGridSpec(
            num_scalar_prefetch=1,
            grid=(steps,),
            in_specs=[
                pl.BlockSpec(memory_space=pl.ANY),
                pl.BlockSpec((1, size), lambda i, *_: (0, 0)),
                pl.BlockSpec((size // 2, piece), lambda i, *_: (0, i)),
                pl.BlockSpec(sky, lambda i, *_: (i, 0, 0)),
                pl.BlockSpec(sky, lambda i, *_: (i, 1, 0)),
            ],
            out_specs=pl.BlockSpec((rows, pixels), lambda i, *_: (0, 0)),
            scratch_shapes=[
                pltpu.SMEM((1, LANES), jnp.int32),
                pltpu.SMEM((groups - 1, LANES), jnp.int32),
                pltpu.VMEM((groups - 1, LANES), jnp.int32),
                dma((2,)),
                dma((groups - 1,)),
                dma((groups - 1,)),
                pltpu.VMEM((8, size), jnp.float32),
                pltpu.VMEM((blocks, width, pixels), jnp.bfloat16),
                pltpu.VMEM((width // LANES, size, LANES), jnp.float32),
                pltpu.VMEM((shards, chips, 2, rows, pixels), jnp.bfloat16),
                pltpu.VMEM((shards, chips, rows, pixels), jnp.bfloat16),
                pltpu.VMEM((shards, chips - 1, rows, pixels), jnp.bfloat16),
                pltpu.VMEM((shards, chips - 1, rows, pixels), jnp.bfloat16),
                pltpu.VMEM((shards, rows, pixels), jnp.float32),
                pltpu.VMEM((shards - 1, rows, pixels), jnp.bfloat16),
                pltpu.VMEM((shards - 1, rows, pixels), jnp.bfloat16),
                dma((shards,)),
                dma((shards,)),
                dma((shards, chips - 1)),
                dma((shards, chips - 1)),
                dma((shards - 1,)),
                dma((shards - 1,)),
            ],
        ),
        compiler_params=pltpu.CompilerParams(
            collective_id=0, has_side_effects=True, vmem_limit_bytes=48 << 20
        ),
        name="stack_stamps",
    )(by_column, lists.reshape(1, LANES), delay_gain.reshape(1, size), cosine_table(size), sky_map, sky_map)
    return out[None]


def solution(mesh):
    in_specs = (
        P("chan", "pix", None),
        P("pix"),
        P("pix", "chan", None, None),
        P("pix", "chan", None, None),
        P(),
        P(),
    )
    run = functools.partial(body, groups=mesh.shape["chan"], shards=mesh.shape["pix"])
    return jax.shard_map(run, mesh=mesh, in_specs=in_specs, out_specs=P("pix", "chan", None), check_vma=False)
```

```python
import functools

import jax
import jax.numpy as jnp
import numpy as np
from jax import lax
from jax.experimental import pallas as pl
from jax.experimental.pallas import tpu as pltpu
from jax.sharding import PartitionSpec as P

MESH = pl.DeviceIdType.MESH
STEP = 32
LANES = 128
LAG1 = 1
LAG2 = 3


def cosine_table(size):
    mode = np.arange(size // 2)[:, None]
    angle = 2.0 * np.pi * ((mode * np.arange(size)[None, :]) % size) / size
    return (np.cos(angle) / size).astype(np.float32)


def filter_piece(gain_ref, table_ref, first):
    size = gain_ref.shape[1]
    half = size // 2
    piece = table_ref.shape[1]
    gain = jnp.broadcast_to(gain_ref[...], (8, size))
    even = gain[:, :half]
    odd = gain[:, half:]
    mode = lax.broadcasted_iota(jnp.int32, (8, half), 1)
    row = lax.broadcasted_iota(jnp.int32, (8, half), 0)
    odd = jnp.where(mode == 0, 0.0, odd)
    minus = jnp.where(mode == 0, 0.0, even - odd)
    gains = jnp.where(row == 0, even + odd, minus)
    out = jnp.dot(gains, table_ref[...], precision=lax.Precision.HIGHEST, preferred_element_type=jnp.float32)
    at = lax.broadcasted_iota(jnp.int32, (8, piece), 1) + first
    sign = jnp.where(lax.rem(at, 2) == 0, 1.0 / size, -1.0 / size)
    top = lax.broadcasted_iota(jnp.int32, (8, piece), 0) == 0
    return out + jnp.where(top, gain[:, half : half + 1] * sign, 0.0)


def resolve_kernel(shards, slots, owner_s, ranks_s, starts_s, out_s, table):
    c = lax.axis_index("chan")

    def fill(b, count):
        table[count] = b
        return count + (owner_s[b] == c).astype(jnp.int32)

    count = lax.fori_loop(0, owner_s.shape[0], fill, jnp.int32(0))
    for q in range(shards):
        for s in range(slots):
            rank = ranks_s[q * slots + s]
            live = (rank >= 0) & (rank < count)
            out_s[q * slots + s] = jnp.where(live, table[jnp.where(live, rank, 0)], -1)
            out_s[(shards + q) * slots + s] = starts_s[q * slots + s]


def fill_filter(first, kernels_ref, filt):
    size = kernels_ref.shape[1]
    halves = filt.shape[0]
    row = lax.broadcasted_iota(jnp.int32, (8, size), 0)
    back = lax.rem(size - first, size)
    diff = pltpu.roll(jnp.broadcast_to(kernels_ref[0:1, :], (8, size)), back, 1)
    add = pltpu.roll(jnp.broadcast_to(kernels_ref[1:2, :], (8, size)), back, 1)
    diff_rows, add_rows = diff, add
    for i in range(1, 8):
        diff_rows = jnp.where(row == i, pltpu.roll(diff, i, 1), diff_rows)
        add_rows = jnp.where(row == i, pltpu.roll(add, size - i, 1), add_rows)
    lanes = size // LANES
    for v in range(LANES // 8):
        right = pltpu.roll(diff_rows, 8 * v, 1) if v else diff_rows
        left = pltpu.roll(add_rows, size - 8 * v, 1) if v else add_rows
        for u in range(lanes):
            for h in range(halves):
                a = (h - u) % lanes
                b = (h + u) % lanes
                rows = right[:, a * LANES : (a + 1) * LANES] + left[:, b * LANES : (b + 1) * LANES]
                rows = rows.astype(jnp.bfloat16).astype(jnp.float32)
                filt[h, u * LANES + 8 * v : u * LANES + 8 * v + 8, :] = rows


def stack_kernel(
    groups, shards, slots, stamp, over_s, lists_ref, gain_ref, table_ref, sky_a, sky_b, out_ref,
    own_s, peers_s, peers, local, send_l, recv_l, kernels_ref, held, filt, part, pair, mid1, near, keep, mid2, far, send0, recv0, send1, recv1, send2, recv2,
):
    step = pl.program_id(0)
    width, pixels = held.shape[1:]
    chips = groups // 2
    rows = stamp // groups
    column = shards * slots
    k = lax.axis_index("chan")
    p = lax.axis_index("pix")
    x = k // 2
    core = lax.rem(k, 2)
    other = 1 - core

    def to_peer(e):
        return pltpu.make_async_remote_copy(
            src_ref=lists_ref,
            dst_ref=peers.at[pl.ds(e - 1, 1)],
            send_sem=send_l.at[e - 1],
            recv_sem=recv_l.at[e - 1],
            device_id=(lax.rem(k + e, groups), p),
            device_id_type=MESH,
        )

    own_lists = pltpu.make_async_copy(lists_ref, own_s, local.at[0])
    peer_lists = pltpu.make_async_copy(peers, peers_s, local.at[1])

    @pl.when(step == 0)
    def _():
        barrier = pltpu.get_barrier_semaphore()
        for e in range(1, groups):
            pl.semaphore_signal(barrier, inc=1, device_id=(lax.rem(k + e, groups), p), device_id_type=MESH)
        for d in range(1, shards):
            pl.semaphore_signal(barrier, inc=1, device_id=(k, lax.rem(p + d, shards)), device_id_type=MESH)

    @pl.when(step == 2)
    def _():
        pl.semaphore_wait(pltpu.get_barrier_semaphore(), groups + shards - 2)
        own_lists.start()
        for e in range(1, groups):
            to_peer(e).start()

    piece = table_ref.shape[1]
    lane = pl.multiple_of(step * piece, piece)
    kernels_ref[:, pl.ds(lane, piece)] = filter_piece(gain_ref, table_ref, lane)

    half = sky_a.shape[1]
    for i in range(sky_a.shape[0] // 16):
        here = pl.multiple_of(step * sky_a.shape[0] + 16 * i, 16)
        held[:half, pl.ds(here, 16), :] = jnp.swapaxes(sky_a[16 * i : 16 * i + 16], 0, 1)
        held[half:, pl.ds(here, 16), :] = jnp.swapaxes(sky_b[16 * i : 16 * i + 16], 0, 1)

    def to_core(i):
        return pltpu.make_async_remote_copy(
            src_ref=part.at[i, :, other],
            dst_ref=pair.at[i],
            send_sem=send0.at[i],
            recv_sem=recv0.at[i],
            device_id=(x * 2 + other, p),
            device_id_type=MESH,
        )

    def to_chip(i, j):
        return pltpu.make_async_remote_copy(
            src_ref=mid1.at[i, j - 1],
            dst_ref=near.at[i, j - 1],
            send_sem=send1.at[i, j - 1],
            recv_sem=recv1.at[i, j - 1],
            device_id=(lax.rem(x + j, chips) * 2 + core, p),
            device_id_type=MESH,
        )

    def to_shard(i):
        return pltpu.make_async_remote_copy(
            src_ref=mid2.at[i],
            dst_ref=far.at[i],
            send_sem=send2.at[i],
            recv_sem=recv2.at[i],
            device_id=(k, lax.rem(p + 1 + i, shards)),
            device_id_type=MESH,
        )

    def compute(i):
        q = lax.rem(p + 1 + i, shards)
        tile = 256
        for n in range(pixels // tile):
            total = jnp.zeros((stamp, tile), jnp.float32)
            for e in range(groups):
                c = lax.rem(k + groups - e, groups)
                for s in range(slots):
                    at = q * slots + s
                    block = peers_s[e - 1, at] if e else own_s[0, at]
                    first = peers_s[e - 1, column + at] if e else own_s[0, column + at]
                    weight = jnp.where(block >= 0, over_s[c * column + at], 0.0)
                    parts = [filt[h, pl.ds(first, stamp), :] for h in range(width // LANES)]
                    cut = jnp.concatenate(parts, axis=1).astype(jnp.bfloat16)
                    columns = held[jnp.maximum(block, 0), :, n * tile : (n + 1) * tile]
                    total += weight * jnp.dot(cut, columns, preferred_element_type=jnp.float32)
            total = total.astype(jnp.bfloat16).reshape(chips, 2, rows, tile)
            part[i, :, :, :, n * tile : (n + 1) * tile] = total

    def pair_sum(i, j):
        to = lax.rem(x + j, chips)
        return part[i, to, core].astype(jnp.float32) + pair[i, to].astype(jnp.float32)

    def chip_stage(i):
        to_core(i).wait_recv()
        for j in range(1, chips):
            mid1[i, j - 1] = pair_sum(i, j).astype(jnp.bfloat16)
            to_chip(i, j).start()
        keep[i] = pair_sum(i, 0)

    def shard_sum(i):
        total = keep[i]
        for j in range(1, chips):
            to_chip(i, j).wait_recv()
            total += near[i, j - 1].astype(jnp.float32)
        return total

    @pl.when(step == pl.num_programs(0) - 1)
    def _():
        for e in range(1, groups):
            to_peer(e).wait_recv()
        peer_lists.start()
        fill_filter(k * width, kernels_ref, filt)
        own_lists.wait()
        peer_lists.wait()

        @pl.loop(0, shards + LAG2 - 1)
        def _(i):
            @pl.when(i < shards)
            def _():
                compute(i)
                to_core(i).start()

            @pl.when((i >= LAG1) & (i < shards + LAG1))
            def _():
                chip_stage(i - LAG1)

            @pl.when(i >= LAG2)
            def _():
                mid2[i - LAG2] = shard_sum(i - LAG2).astype(jnp.bfloat16)
                to_shard(i - LAG2).start()

        out_ref[...] = shard_sum(shards - 1)
        for i in range(shards - 1):
            to_shard(i).wait_recv()
            out_ref[...] += far[i].astype(jnp.float32)
        for e in range(1, groups):
            to_peer(e).wait_send()
        for i in range(shards):
            to_core(i).wait_send()
            for j in range(1, chips):
                to_chip(i, j).wait_send()
            if i < shards - 1:
                to_shard(i).wait_send()


def body(sky_map, owner, stamp_block, chan_start, overdensity, delay_gain, *, groups, shards):
    p = lax.axis_index("pix")
    width, blocks, pixels = sky_map.shape
    stamp = 128
    chips = groups // 2
    rows = stamp // groups
    slots = stamp_block.shape[3]

    smem = pl.BlockSpec(memory_space=pltpu.SMEM)
    lists = pl.pallas_call(
        functools.partial(resolve_kernel, shards, slots),
        out_shape=jax.ShapeDtypeStruct((LANES,), jnp.int32),
        in_specs=[smem] * 3,
        out_specs=smem,
        scratch_shapes=[pltpu.SMEM((blocks + 1,), jnp.int32)],
        name="resolve_slots",
    )(owner, stamp_block.reshape(-1), chan_start.reshape(-1))
    by_column = lax.dynamic_index_in_dim(overdensity, p, 0, False).reshape(-1)
    step = min(STEP, width)
    steps = width // step
    size = delay_gain.shape[0]
    piece = size // steps

    dma = pltpu.SemaphoreType.DMA
    sky = (step, blocks // 2, pixels)
    out = pl.pallas_call(
        functools.partial(stack_kernel, groups, shards, slots, stamp),
        out_shape=jax.ShapeDtypeStruct((rows, pixels), jnp.float32),
        grid_spec=pltpu.PrefetchScalarGridSpec(
            num_scalar_prefetch=1,
            grid=(steps,),
            in_specs=[
                pl.BlockSpec(memory_space=pl.ANY),
                pl.BlockSpec((1, size), lambda i, *_: (0, 0)),
                pl.BlockSpec((size // 2, piece), lambda i, *_: (0, i)),
                pl.BlockSpec(sky, lambda i, *_: (i, 0, 0)),
                pl.BlockSpec(sky, lambda i, *_: (i, 1, 0)),
            ],
            out_specs=pl.BlockSpec((rows, pixels), lambda i, *_: (0, 0)),
            scratch_shapes=[
                pltpu.SMEM((1, LANES), jnp.int32),
                pltpu.SMEM((groups - 1, LANES), jnp.int32),
                pltpu.VMEM((groups - 1, LANES), jnp.int32),
                dma((2,)),
                dma((groups - 1,)),
                dma((groups - 1,)),
                pltpu.VMEM((8, size), jnp.float32),
                pltpu.VMEM((blocks, width, pixels), jnp.bfloat16),
                pltpu.VMEM((width // LANES, size, LANES), jnp.float32),
                pltpu.VMEM((shards, chips, 2, rows, pixels), jnp.bfloat16),
                pltpu.VMEM((shards, chips, rows, pixels), jnp.bfloat16),
                pltpu.VMEM((shards, chips - 1, rows, pixels), jnp.bfloat16),
                pltpu.VMEM((shards, chips - 1, rows, pixels), jnp.bfloat16),
                pltpu.VMEM((shards, rows, pixels), jnp.float32),
                pltpu.VMEM((shards - 1, rows, pixels), jnp.bfloat16),
                pltpu.VMEM((shards - 1, rows, pixels), jnp.bfloat16),
                dma((shards,)),
                dma((shards,)),
                dma((shards, chips - 1)),
                dma((shards, chips - 1)),
                dma((shards - 1,)),
                dma((shards - 1,)),
            ],
        ),
        compiler_params=pltpu.CompilerParams(
            collective_id=0, has_side_effects=True, vmem_limit_bytes=48 << 20
        ),
        name="stack_stamps",
    )(by_column, lists.reshape(1, LANES), delay_gain.reshape(1, size), cosine_table(size), sky_map, sky_map)
    return out[None]


def solution(mesh):
    in_specs = (
        P("chan", "pix", None),
        P("pix"),
        P("pix", "chan", None, None),
        P("pix", "chan", None, None),
        P(),
        P(),
    )
    run = functools.partial(body, groups=mesh.shape["chan"], shards=mesh.shape["pix"])
    return jax.shard_map(run, mesh=mesh, in_specs=in_specs, out_specs=P("pix", "chan", None), check_vma=False)
```
